32 devices in a mesh: row: 8 (over z, y), col: 4 (over x, core).
Axes of the slice: x: 2, y: 2, z: 4, core: 2. Of those that a mesh axis runs over, the one named last changes fastest.
Arguments:
- rhs: float32 [32768, 256], P(('row', 'col')), may hold values from -8 to 8
- front_factor: float32 [32768, 1024], P(('row', 'col')), may hold values from -1 to 4, as said below
- coupling: bfloat16 [57344, 1024], P(('row', 'col')), may hold values from -0.1875 to 0.1875
- bound_count: int32 [32], P(('row', 'col')), may hold values from 448 to 1792, as said below
- sep_owner: int32 [32, 16], P(('row', 'col')), may hold values from 0 to 31, as said below
- sep_index: int32 [32, 1792], P(('row', 'col')), may hold values from 0 to 511
- sep_rhs: float32 [16384, 256], P(('row', 'col')), may hold values from -6 to 6
- sep_factor: float32 [16384, 512], P(('row', 'col')), may hold values from -1 to 4, as said below
- cell_weight: float32 [4096, 8], P(('row', 'col')), may hold values from 0.02 to 0.3
- cell_pivot: int32 [4096, 8], P(('row', 'col')), may hold values from 0 to 1023
Outputs:
- sep_potential: float32 [16384, 256], P(('row', 'col'))
- hess: float32 [4096, 4096], P('row', 'col')
The draws below stay inside these ranges and needn't reach their ends.
Inputs may be any that keep to these rules, and one draw needn't show every extreme that they name: `front_factor`: each block of 1024 rows is lower triangular with diagonal entries 1 or more. `sep_factor`: each block of 512 rows is lower triangular with diagonal entries 1 or more. `bound_count`: some front has all 1792 boundary rows live. `sep_owner`: each row names 16 distinct separator blocks.
All inputs are finite; a program needn't handle non-finite values.
Results may differ from the reference program's by a relative error of at most 0.0031.
Values may be sent and summed in bfloat16 or wider, within the bound.
A program may use at most 128 MiB of HBM per device.

```python
import math
import jax
import jax.numpy as jnp
from jax import lax

P_SIZE = 1024
B = 1792
S = 256
SEP = 512
CELL_DEV = 128
NNZ = 8
FRONTS = 32
CELLS = 4096
N_ROW = 8
N_COL = 4


def lower_blocks(key, count, order):
    first, second = jax.random.split(key)
    diagonal = jax.random.uniform(first, (count, order), jnp.float32, 1.0, 2.0)
    spread = jnp.clip(jax.random.normal(second, (count, order, order), jnp.float32), -6.0, 6.0)
    lower = jnp.tril(spread * (0.5 / math.sqrt(order)), -1)
    whole = lower + diagonal[:, :, None] * jnp.eye(order, dtype=jnp.float32)[None, :, :]
    return whole.reshape(count * order, order)


def draw_rhs(key, part):
    first, second = jax.random.split(jax.random.fold_in(key, 11))
    common = jnp.clip(jax.random.normal(first, (1, S), jnp.float32), -3.0, 3.0)
    noise = jax.random.normal(second, (FRONTS * P_SIZE, S), jnp.float32)
    return jnp.clip(common + noise, -8.0, 8.0)


def draw_front_factor(key, part):
    return lower_blocks(jax.random.fold_in(key, 23), FRONTS, P_SIZE)


def draw_sep_factor(key, part):
    return lower_blocks(jax.random.fold_in(key, 37), FRONTS, SEP)


def draw_bound_count(key, part):
    first, second = jax.random.split(jax.random.fold_in(key, 41))
    counts = jax.random.randint(first, (FRONTS,), B // 4, B + 1, dtype=jnp.int32)
    chosen = jax.random.randint(second, (), 0, FRONTS, dtype=jnp.int32)
    return counts.at[chosen].set(B)


def draw_sep_owner(key, part):
    keys = jax.random.split(jax.random.fold_in(key, 53), FRONTS)
    orders = jax.vmap(lambda single: jax.random.permutation(single, FRONTS))(keys)
    return orders[:, :FRONTS // 2].astype(jnp.int32)


def set_ends(entries, own_key, smallest, high):
    shape = entries.shape
    spot = [jax.random.randint(jax.random.fold_in(own_key, axis), (), 0, shape[axis]) for axis in range(len(shape))]
    entries = entries.at[tuple(spot)].set(smallest)
    longest = shape.index(max(shape))
    spot[longest] = (spot[longest] + 1) % shape[longest]
    return entries.at[tuple(spot)].set(high)


def shard_levels(key, extent, cuts, smallest, largest):
    factor_of, own = 1.0, jax.random.fold_in(key, 6)
    for axis_at, shards_of in cuts:
        heights = jnp.exp(jax.random.uniform(jax.random.fold_in(own, axis_at), (shards_of,), jnp.float32, smallest / len(cuts), largest / len(cuts)))
        factor_of = factor_of * jnp.repeat(heights, extent[axis_at] // shards_of).reshape([-1 if axis == axis_at else 1 for axis in range(len(extent))])
    return factor_of


def gaussian(own_key, shape, deviation, bound, shards=(), kind=jnp.bfloat16):
    drawn = jax.random.normal(own_key, shape, jnp.float32) * deviation
    if len(shards) > 0:
        drawn = shard_levels(own_key, shape, shards, -0.22, 0.18) * drawn
    return jnp.clip(drawn, min=-bound, max=bound).astype(kind)


def setup_inputs(seed: int = 0) -> dict:
    seeds = jax.random.split(jax.random.key(seed), 11)
    return {
        "rhs": draw_rhs(jax.random.fold_in(seeds[10], 71), 0),
        "front_factor": draw_front_factor(jax.random.fold_in(seeds[10], 71), 0),
        "coupling": gaussian(seeds[2], (FRONTS * B, P_SIZE), P_SIZE ** -0.5, 0.1875, ((0, 32),)),
        "bound_count": draw_bound_count(jax.random.fold_in(seeds[10], 71), 0),
        "sep_owner": draw_sep_owner(jax.random.fold_in(seeds[10], 71), 0),
        "sep_index": set_ends(jax.random.randint(seeds[5], (FRONTS, B), 0, SEP), jax.random.fold_in(seeds[5], 1), 0, SEP - 1).astype(jnp.int32),
        "sep_rhs": gaussian(seeds[6], (FRONTS * SEP, S), 1.0, 6.0, ((0, 32),), jnp.float32),
        "sep_factor": draw_sep_factor(jax.random.fold_in(seeds[10], 71), 0),
        "cell_weight": jnp.clip(jnp.exp(math.log(0.3) - 2.7080503 * jax.random.uniform(seeds[8], (CELLS, NNZ), jnp.float32) ** shard_levels(seeds[8], (CELLS, NNZ), ((0, 32),), -0.2, 0.2)), 0.02, 0.3),
        "cell_pivot": set_ends(jax.random.randint(seeds[9], (CELLS, NNZ), 0, P_SIZE), jax.random.fold_in(seeds[9], 1), 0, P_SIZE - 1).astype(jnp.int32),
    }


def front_solve(factor, right):
    half_way = jax.scipy.linalg.solve_triangular(factor, right, lower=True)
    return jax.scipy.linalg.solve_triangular(factor, half_way, trans=1, lower=True)

def reference(rhs, front_factor, coupling, bound_count, sep_owner, sep_index, sep_rhs, sep_factor, cell_weight, cell_pivot):
    fronts = N_ROW * N_COL
    halves = fronts // 2
    slots = B // halves
    factors = front_factor.reshape(fronts, P_SIZE, P_SIZE)
    rights = rhs.reshape(fronts, P_SIZE, S)
    blocks = coupling.reshape(fronts, B, P_SIZE)
    living = jnp.arange(B, dtype=jnp.int32)[None, :] < bound_count[:, None]
    live_float = living.astype(jnp.float32)
    live_half = living.astype(jnp.bfloat16)
    slot_owner = jnp.repeat(sep_owner, slots, axis=1)
    global_index = (slot_owner * SEP + sep_index).astype(jnp.int32)

    def forward(inputs):
        factor, right, block, marks = inputs
        solved = front_solve(factor, right).astype(jnp.bfloat16)
        product = jnp.dot(block.astype(jnp.float32), solved.astype(jnp.float32), preferred_element_type=jnp.float32)
        return (product * marks[:, None]).astype(jnp.bfloat16)
    contrib = lax.map(forward, (factors, rights, blocks, live_float))
    totals = jnp.zeros((fronts * SEP, S), jnp.float32).at[global_index.reshape(-1)].add(contrib.reshape(-1, S).astype(jnp.float32))
    reduced = (sep_rhs - totals).reshape(fronts, SEP, S)
    sep_blocks = sep_factor.reshape(fronts, SEP, SEP)

    def separator(inputs):
        return front_solve(inputs[0], inputs[1])
    sep_potential = lax.map(separator, (sep_blocks, reduced)).reshape(fronts * SEP, S)
    sep_half = sep_potential.astype(jnp.bfloat16)
    weights = cell_weight.reshape(fronts, CELL_DEV, NNZ)
    pivots = cell_pivot.reshape(fronts, CELL_DEV, NNZ)

    def backward(inputs):
        factor, right, block, marks, index, weight, pivot = inputs
        values = sep_half[index] * marks[:, None]
        lifted = lax.dot_general(block.astype(jnp.float32), values.astype(jnp.float32), (((0,), (0,)), ((), ())), preferred_element_type=jnp.float32)
        potential = front_solve(factor, right - lifted)
        picked = potential[pivot]
        return jnp.sum(weight[:, :, None] * picked, axis=1).astype(jnp.bfloat16)
    field = lax.map(backward, (factors, rights, blocks, live_half, global_index, weights, pivots)).reshape(fronts * CELL_DEV, S)
    colfield = field.reshape(N_ROW, N_COL, CELL_DEV, S).transpose(1, 0, 2, 3).reshape(fronts * CELL_DEV, S)
    gram = lax.dot_general(field.astype(jnp.float32), colfield.astype(jnp.float32), (((1,), (1,)), ((), ())), preferred_element_type=jnp.float32) * (1.0 / S)
    return (sep_potential, gram * gram)
```

```python
import functools

import jax
import jax.numpy as jnp
from jax import lax
from jax.experimental import pallas as pl
from jax.experimental.pallas import tpu as pltpu
from jax.sharding import PartitionSpec as P

F32 = jnp.float32
BF16 = jnp.bfloat16
NN = (((1,), (0,)), ((), ()))
NT = (((1,), (1,)), ((), ()))
VMEM_LIMIT = 63 * 1024 * 1024


def split(value):
    high = value.astype(BF16)
    return high, (value - high.astype(F32)).astype(BF16)


def dot(left, right, dims):
    return lax.dot_general(left, right, dims, preferred_element_type=F32)


def dot3(left, right, dims=NN):
    return dot(left[0], right[0], dims) + (dot(left[0], right[1], dims) + dot(left[1], right[0], dims))


def invert(factor_ref, high_ref, low_ref, work_ref):
    order = factor_ref.shape[0]
    base = work_ref.shape[1]
    count = order // base
    rows = lax.broadcasted_iota(jnp.int32, (base, base), 0)
    cols = lax.broadcasted_iota(jnp.int32, (base, base), 1)
    differ = rows ^ cols
    below = rows > cols
    high_ref[...] = jnp.zeros_like(high_ref)
    low_ref[...] = jnp.zeros_like(low_ref)

    def diagonal(block):
        return factor_ref[pl.ds(block * base, base), pl.ds(block * base, base)]

    for block in range(count):
        part = diagonal(block)
        only = jnp.where(differ == 0, part, 0.0)
        down = 1.0 / jnp.sum(only, axis=1, keepdims=True)
        across = 1.0 / jnp.sum(only, axis=0, keepdims=True)
        pairs = jnp.where(below & (differ == 1), (part * down) * across, 0.0)
        work_ref[block] = jnp.where(differ == 0, jnp.broadcast_to(down, part.shape), -pairs)
    size = 2
    while size < base:
        inside = below & (differ >= size) & (differ < 2 * size)
        for block in range(count):
            outer = split(jnp.where(inside, diagonal(block), 0.0))
            held = work_ref[block]
            parts = split(held)
            step = split(dot3(outer, parts))
            work_ref[block] = held - dot3(parts, step)
        size *= 2
    for block in range(count):
        spot = pl.ds(block * base, base)
        high, low = split(work_ref[block])
        high_ref[spot, spot] = high
        low_ref[spot, spot] = low
    size = base
    while size < order:
        for start in range(0, order, 2 * size):
            first, second = pl.ds(start, size), pl.ds(start + size, size)
            outer = split(factor_ref[second, first])
            step = split(dot3(outer, (high_ref[first, first], low_ref[first, first])))
            high, low = split(-dot3((high_ref[second, second], low_ref[second, second]), step))
            high_ref[second, first] = high
            low_ref[second, first] = low
        size *= 2


def both(parts_ref):
    return parts_ref[0][...], parts_ref[1][...]


def turned_solve(turned, high_ref, low_ref):
    inverse = (high_ref[...], low_ref[...])
    half_way = split(dot3(split(turned), inverse, NT))
    return dot3(half_way, inverse, NN)


def front_kernel(count_ref, owner_ref, factor_ref, rhs_ref, coupling_ref, out_ref, high_ref, low_ref, work_ref, contrib_ref):
    invert(factor_ref, high_ref, low_ref, work_ref)
    solved = turned_solve(rhs_ref[...].T, high_ref, low_ref).astype(BF16)
    product = dot(coupling_ref[...], solved, NT)
    rows = lax.broadcasted_iota(jnp.int32, product.shape, 0)
    contrib_ref[...] = jnp.where(rows < count_ref[0], product, 0.0).astype(BF16)
    out_ref[...] = jnp.zeros_like(out_ref)
    slots = out_ref.shape[1]
    for half in range(owner_ref.shape[1]):
        out_ref[owner_ref[0, half]] = contrib_ref[pl.ds(half * slots, slots), :]


def separator_inverse_kernel(factor_ref, high_ref, low_ref, turned_high_ref, turned_low_ref, work_ref):
    invert(factor_ref, high_ref, low_ref, work_ref)
    turned_high_ref[...] = high_ref[...].T
    turned_low_ref[...] = low_ref[...].T


def owner_kernel(row_ref, column_ref, received_ref, rhs_ref, high_ref, low_ref, turned_high_ref, turned_low_ref, out_ref, reply_ref):
    size = rhs_ref.shape[0]
    total = row_ref.shape[1]
    selector = (lax.broadcasted_iota(jnp.int32, (size, total), 0) == row_ref[...]).astype(F32).astype(BF16)
    reduced = rhs_ref[...] - dot(selector, received_ref[...], NN)
    half_way = split(dot3((high_ref[...], low_ref[...]), split(reduced)))
    potential = dot3((turned_high_ref[...], turned_low_ref[...]), half_way)
    out_ref[...] = potential
    picker = (lax.broadcasted_iota(jnp.int32, (total, size), 1) == column_ref[...]).astype(F32).astype(BF16)
    reply_ref[...] = dot(picker, potential.astype(BF16), NN).astype(BF16)


def back_kernel(count_ref, owner_ref, returned_ref, rhs_ref, coupling_ref, high_ref, low_ref, weight_ref, pivot_ref, field_ref, values_ref):
    slots = returned_ref.shape[1]
    for half in range(owner_ref.shape[1]):
        values_ref[pl.ds(half * slots, slots), :] = returned_ref[owner_ref[0, half]]
    values = values_ref[...]
    rows = lax.broadcasted_iota(jnp.int32, values.shape, 0)
    values = jnp.where(rows < count_ref[0], values.astype(F32), 0.0)
    lifted = dot(values.T.astype(BF16), coupling_ref[...], NN)
    potential = turned_solve(rhs_ref[...].T - lifted, high_ref, low_ref)
    shape = (weight_ref.shape[0], rhs_ref.shape[0])
    spots = lax.broadcasted_iota(jnp.int32, shape, 1)
    spread = jnp.zeros(shape, F32)
    for near in range(weight_ref.shape[1]):
        spread += jnp.where(spots == pivot_ref[:, near : near + 1], weight_ref[:, near : near + 1], 0.0)
    field_ref[...] = dot3(split(spread), split(potential), NT).astype(BF16)


def call(kernel, out_shape, in_specs, scratch, flops, moved, **more):
    outs = jax.tree.map(lambda _: pl.BlockSpec(memory_space=pltpu.VMEM), out_shape)
    return pl.pallas_call(
        kernel,
        out_shape=out_shape,
        in_specs=in_specs,
        out_specs=outs,
        scratch_shapes=scratch,
        cost_estimate=pl.CostEstimate(flops=flops, bytes_accessed=moved, transcendentals=0),
        compiler_params=pltpu.CompilerParams(vmem_limit_bytes=VMEM_LIMIT, **more),
    )


def local(
    rhs,
    front_factor,
    coupling,
    bound_count,
    sep_owner,
    sep_index,
    sep_rhs,
    sep_factor,
    cell_weight,
    cell_pivot,
):
    fronts = lax.axis_size("row") * lax.axis_size("col")
    bound = coupling.shape[0]
    pivots, sources = rhs.shape
    sep_size = sep_rhs.shape[0]
    halves = sep_owner.shape[1]
    slots = bound // halves
    shape = jax.ShapeDtypeStruct
    smem = pl.BlockSpec(memory_space=pltpu.SMEM)
    vmem = pl.BlockSpec(memory_space=pltpu.VMEM)
    base = 256
    owners = sep_owner[0]
    out_index = (
        jnp.full((fronts, slots), -1, jnp.int32).at[owners].set(sep_index[0].reshape(halves, slots))
    )
    in_index = lax.all_to_all(out_index, ("row", "col"), split_axis=0, concat_axis=0, tiled=True)
    outgoing, high, low = call(
        front_kernel,
        (
            shape((fronts, slots, sources), BF16),
            shape((pivots, pivots), BF16),
            shape((pivots, pivots), BF16),
        ),
        [smem, smem, vmem, vmem, vmem],
        [pltpu.VMEM((pivots // base, base, base), F32), pltpu.VMEM((bound, sources), BF16)],
        10**10,
        10**7,
    )(bound_count, sep_owner, front_factor, rhs, coupling)
    incoming = lax.all_to_all(outgoing, ("row", "col"), split_axis=0, concat_axis=0, tiled=True)
    received = incoming.reshape(fronts * slots, sources)
    inverse = call(
        separator_inverse_kernel,
        tuple(shape((sep_size, sep_size), BF16) for _ in range(4)),
        [vmem],
        [pltpu.VMEM((sep_size // base, base, base), F32)],
        10**10,
        10**7,
    )(sep_factor)
    sep_potential, replies = call(
        owner_kernel,
        (shape((sep_size, sources), F32), shape((fronts * slots, sources), BF16)),
        [vmem] * 8,
        [],
        10**9,
        10**7,
    )(in_index.reshape(1, fronts * slots), in_index.reshape(fronts * slots, 1), received, sep_rhs, *inverse)
    returned = lax.all_to_all(
        replies.reshape(fronts, slots, sources),
        ("row", "col"),
        split_axis=0,
        concat_axis=0,
        tiled=True,
    )
    field = call(
        back_kernel,
        shape((cell_weight.shape[0], sources), BF16),
        [smem, smem] + [vmem] * 7,
        [pltpu.VMEM((bound, sources), BF16)],
        10**9,
        10**7,
    )(bound_count, sep_owner, returned, rhs, coupling, high, low, cell_weight, cell_pivot)
    scale = 1.0 / sources
    row_tile = lax.all_gather(field, "col", axis=0, tiled=True)
    gram = (
        lax.dot_general(
            row_tile,
            lax.all_gather(field, "row", axis=0, tiled=True),
            NT,
            preferred_element_type=jnp.float32,
        )
        * scale
    )
    return (sep_potential, gram * gram)


def solution(mesh):
    both_axes = P(("row", "col"), None)
    placed = (both_axes, both_axes, both_axes, P(("row", "col"))) + (both_axes,) * 6
    return jax.shard_map(
        local,
        mesh=mesh,
        in_specs=placed,
        out_specs=(both_axes, P("row", "col")),
        check_vma=False,
    )
```

```python
import functools

import jax
import jax.numpy as jnp
from jax import lax
from jax.experimental import pallas as pl
from jax.experimental.pallas import tpu as pltpu
from jax.sharding import PartitionSpec as P

F32 = jnp.float32
BF16 = jnp.bfloat16
NN = (((1,), (0,)), ((), ()))
NT = (((1,), (1,)), ((), ()))
VMEM_LIMIT = 63 * 1024 * 1024


def split(value):
    high = value.astype(BF16)
    return high, (value - high.astype(F32)).astype(BF16)


def dot(left, right, dims):
    return lax.dot_general(left, right, dims, preferred_element_type=F32)


def dot3(left, right, dims=NN):
    return dot(left[0], right[0], dims) + (dot(left[0], right[1], dims) + dot(left[1], right[0], dims))


def invert(factor_ref, high_ref, low_ref, work_ref):
    order = factor_ref.shape[0]
    base = work_ref.shape[1]
    count = order // base
    rows = lax.broadcasted_iota(jnp.int32, (base, base), 0)
    cols = lax.broadcasted_iota(jnp.int32, (base, base), 1)
    differ = rows ^ cols
    below = rows > cols
    high_ref[...] = jnp.zeros_like(high_ref)
    low_ref[...] = jnp.zeros_like(low_ref)

    def diagonal(block):
        return factor_ref[pl.ds(block * base, base), pl.ds(block * base, base)]

    for block in range(count):
        part = diagonal(block)
        only = jnp.where(differ == 0, part, 0.0)
        down = 1.0 / jnp.sum(only, axis=1, keepdims=True)
        across = 1.0 / jnp.sum(only, axis=0, keepdims=True)
        pairs = jnp.where(below & (differ == 1), (part * down) * across, 0.0)
        work_ref[block] = jnp.where(differ == 0, jnp.broadcast_to(down, part.shape), -pairs)
    size = 2
    while size < base:
        inside = below & (differ >= size) & (differ < 2 * size)
        for block in range(count):
            outer = split(jnp.where(inside, diagonal(block), 0.0))
            held = work_ref[block]
            parts = split(held)
            step = split(dot3(outer, parts))
            work_ref[block] = held - dot3(parts, step)
        size *= 2
    for block in range(count):
        spot = pl.ds(block * base, base)
        high, low = split(work_ref[block])
        high_ref[spot, spot] = high
        low_ref[spot, spot] = low
    size = base
    while size < order:
        for start in range(0, order, 2 * size):
            first, second = pl.ds(start, size), pl.ds(start + size, size)
            outer = split(factor_ref[second, first])
            step = split(dot3(outer, (high_ref[first, first], low_ref[first, first])))
            high, low = split(-dot3((high_ref[second, second], low_ref[second, second]), step))
            high_ref[second, first] = high
            low_ref[second, first] = low
        size *= 2


def turned_solve(turned, high_ref, low_ref):
    inverse = (high_ref[...], low_ref[...])
    half_way = split(dot3(split(turned), inverse, NT))
    return dot3(half_way, inverse, NN)


MESH = pl.DeviceIdType.MESH


def whole_kernel(
    depth,
    count_ref,
    owner_ref,
    place_ref,
    table_ref,
    factor_ref,
    rhs_ref,
    coupling_ref,
    sep_rhs_ref,
    sep_factor_ref,
    weight_ref,
    pivot_ref,
    sep_out_ref,
    row_out_ref,
    col_out_ref,
    high_ref,
    low_ref,
    work_ref,
    sep_high_ref,
    sep_low_ref,
    sep_work_ref,
    flat_ref,
    contrib_ref,
    index_out_ref,
    index_ref,
    column_ref,
    stage_ref,
    received_ref,
    chain_out_ref,
    up_ref,
    down_ref,
    own_ref,
    halves_ref,
    reply_ref,
    returned_ref,
    index_send,
    index_recv,
    out_send,
    out_recv,
    chain_send,
    up_recv,
    down_recv,
    relay_up_send,
    relay_down_send,
    relay_recv,
    reply_send,
    reply_recv,
    field_send,
    field_recv,
    next_send,
    row_send,
    row_recv,
):
    rows, cols = col_out_ref.shape[0], row_out_ref.shape[0]
    width = rows // depth
    plane = width * cols
    row, col = lax.axis_index("row"), lax.axis_index("col")
    z, y = row // width, row % width
    me = y * cols + col
    halves, slots = owner_ref.shape[1], table_ref.shape[2]
    sep_size = sep_rhs_ref.shape[0]

    def peer(spot):
        return (z * width + spot // cols, spot % cols)

    def level(spot):
        return (spot * width + y, col)

    barrier = pltpu.get_barrier_semaphore()
    for step in range(1, plane):
        pl.semaphore_signal(barrier, inc=1, device_id=peer((me + step) % plane), device_id_type=MESH)
    for step in range(1, depth):
        pl.semaphore_signal(barrier, inc=1, device_id=level((z + step) % depth), device_id_type=MESH)

    def remote(source, target, send, recv, device):
        return pltpu.make_async_remote_copy(
            src_ref=source, dst_ref=target, send_sem=send, recv_sem=recv, device_id=device, device_id_type=MESH
        )

    def index_copy(spot):
        return remote(index_out_ref.at[spot], index_ref.at[me], index_send.at[spot], index_recv.at[me], peer(spot))

    def index_arrival(spot):
        return remote(index_out_ref.at[spot], index_ref.at[spot], index_send.at[spot], index_recv.at[spot], peer(spot))

    def out_copy(high, spot):
        return remote(
            stage_ref.at[high, spot], received_ref.at[high, me], out_send.at[high, spot], out_recv.at[high, me], peer(spot)
        )

    def out_arrival(high, spot):
        return remote(
            stage_ref.at[high, spot], received_ref.at[high, spot], out_send.at[high, spot], out_recv.at[high, spot], peer(spot)
        )

    def up_copy(high):
        return remote(chain_out_ref.at[high], up_ref.at[high], chain_send.at[high], up_recv.at[high], level(z + 1))

    def down_copy(high):
        return remote(chain_out_ref.at[high], down_ref.at[high], chain_send.at[high], down_recv.at[high], level(z - 1))

    def relay_up(high):
        return remote(halves_ref.at[high], halves_ref.at[high], relay_up_send.at[high], relay_recv.at[high], level(z + 1))

    def relay_down(high):
        return remote(halves_ref.at[high], halves_ref.at[high], relay_down_send.at[high], relay_recv.at[high], level(z - 1))

    def reply_copy(high, spot):
        return remote(
            reply_ref.at[high, spot], returned_ref.at[high * plane + me], reply_send.at[high, spot], reply_recv.at[high, me], peer(spot)
        )

    def reply_arrival(high, spot):
        return remote(
            reply_ref.at[high, spot], returned_ref.at[high * plane + spot], reply_send.at[high, spot], reply_recv.at[high, spot], peer(spot)
        )

    def others(action):
        def step(offset, carry):
            action((me + offset) % plane)
            return carry

        lax.fori_loop(1, plane, step, 0)

    def levels(order, action):
        def step(at, carry):
            spot = order(at)

            @pl.when((spot >= 0) & (spot < depth))
            def _():
                action(spot)

            return carry

        lax.fori_loop(0, 2 * depth - 1, step, 0)

    def far_first(at):
        distance = depth - 1 - at // 2
        return z + distance * (1 - 2 * (at % 2))

    def near_first(at):
        return z + ((at + 1) // 2) * (1 - 2 * (at % 2))

    invert(factor_ref, high_ref, low_ref, work_ref)
    pl.semaphore_wait(barrier, plane + depth - 2)

    def fill_index(spot, carry):
        for high in range(depth):
            index_out_ref[spot, high] = table_ref[place_ref[high * plane + spot]]
        return carry

    lax.fori_loop(0, plane, fill_index, 0)
    others(lambda spot: index_copy(spot).start())
    index_ref[me] = index_out_ref[me]

    turned_rhs = rhs_ref[...].T
    solved = turned_solve(turned_rhs, high_ref, low_ref).astype(BF16)
    product = dot(coupling_ref[...], solved, NT)
    live = lax.broadcasted_iota(jnp.int32, product.shape, 0) < count_ref[0]
    flat_ref[...] = jnp.where(live, product, 0.0).astype(BF16)
    for half in range(halves):
        contrib_ref[half] = flat_ref[pl.ds(half * slots, slots), :]
    contrib_ref[halves] = jnp.zeros(contrib_ref.shape[1:], BF16)

    def send_out(high):
        def one(spot):
            stage_ref[high, spot] = contrib_ref[place_ref[high * plane + spot]]
            out_copy(high, spot).start()

        others(one)
        received_ref[high, me] = contrib_ref[place_ref[high * plane + me]]

    levels(far_first, send_out)
    invert(sep_factor_ref, sep_high_ref, sep_low_ref, sep_work_ref)
    others(lambda spot: index_arrival(spot).wait_recv())
    for high in range(depth):
        column_ref[high] = jnp.concatenate([index_ref[spot, high] for spot in range(plane)], axis=0).T

    def gather_in(high):
        others(lambda spot: out_arrival(high, spot).wait_recv())
        numbers = lax.broadcasted_iota(jnp.int32, (sep_size, slots), 0)
        own_ref[...] = jnp.zeros_like(own_ref)
        for spot in range(plane):
            selector = jnp.where(numbers == index_ref[spot, high], 1.0, 0.0).astype(BF16)
            own_ref[...] += dot(selector, received_ref[high, spot], NN)

        @pl.when((high >= z) & (z > 0))
        def _():
            remote(chain_out_ref.at[high], up_ref.at[high], chain_send.at[high], up_recv.at[high], level(z - 1)).wait_recv()
            own_ref[...] += up_ref[high].astype(F32)

        @pl.when((high <= z) & (z < depth - 1))
        def _():
            remote(chain_out_ref.at[high], down_ref.at[high], chain_send.at[high], down_recv.at[high], level(z + 1)).wait_recv()
            own_ref[...] += down_ref[high].astype(F32)

        @pl.when(high != z)
        def _():
            chain_out_ref[high] = own_ref[...].astype(BF16)

        @pl.when(high > z)
        def _():
            up_copy(high).start()

        @pl.when(high < z)
        def _():
            down_copy(high).start()

    levels(far_first, gather_in)
    reduced = (sep_rhs_ref[...] - own_ref[...]).T
    potential = turned_solve(reduced, sep_high_ref, sep_low_ref).T
    sep_out_ref[...] = potential
    halves_ref[z] = potential.astype(BF16)

    def pass_on(high):
        @pl.when(high != z)
        def _():
            remote(halves_ref.at[high], halves_ref.at[high], relay_up_send.at[high], relay_recv.at[high], level((z + 1) % depth)).wait_recv()

        @pl.when((high <= z) & (z < depth - 1))
        def _():
            relay_up(high).start()

        @pl.when((high >= z) & (z > 0))
        def _():
            relay_down(high).start()

        numbers = lax.broadcasted_iota(jnp.int32, (slots, sep_size), 1)
        for spot in range(plane):
            picker = jnp.where(numbers == column_ref[high, :, spot : spot + 1], 1.0, 0.0).astype(BF16)
            reply_ref[high, spot] = dot(picker, halves_ref[high], NN).astype(BF16)

            @pl.when(me != spot)
            def _():
                reply_copy(high, spot).start()

        returned_ref[high * plane + me] = reply_ref[high, me]

    levels(near_first, pass_on)
    shape = (weight_ref.shape[0], rhs_ref.shape[0])
    spots = lax.broadcasted_iota(jnp.int32, shape, 1)
    spread = jnp.zeros(shape, F32)
    for near in range(weight_ref.shape[1]):
        spread += jnp.where(spots == pivot_ref[:, near : near + 1], weight_ref[:, near : near + 1], 0.0)
    levels(near_first, lambda high: others(lambda spot: reply_arrival(high, spot).wait_recv()))
    for half in range(halves):
        flat_ref[pl.ds(half * slots, slots), :] = returned_ref[owner_ref[0, half]]
    values = flat_ref[...]
    live = lax.broadcasted_iota(jnp.int32, values.shape, 0) < count_ref[0]
    values = jnp.where(live, values.astype(F32), 0.0)
    lifted = dot(values.T.astype(BF16), coupling_ref[...], NN)
    potential = turned_solve(rhs_ref[...].T - lifted, high_ref, low_ref)
    field = dot3(split(spread), split(potential), NT).astype(BF16)
    col_out_ref[row] = field
    row_out_ref[col] = field

    def field_copy(step):
        return remote(
            col_out_ref.at[row], col_out_ref.at[row], field_send.at[step], field_recv.at[row], level((z + step) % depth)
        )

    def next_copy(step, turn, high):
        spot = high * width + y
        target = (z * width + (y + turn) % width, col)
        return remote(col_out_ref.at[spot], col_out_ref.at[spot], next_send.at[step, turn], field_recv.at[spot], target)

    def row_copy(step):
        return remote(
            row_out_ref.at[col], row_out_ref.at[col], row_send.at[step], row_recv.at[col], (row, (col + step) % cols)
        )

    def field_arrival(spot):
        return remote(col_out_ref.at[spot], col_out_ref.at[spot], field_send.at[0], field_recv.at[spot], level((z + 1) % depth))

    for step in range(1, depth):
        field_copy(step).start()
    for turn in range(1, width):
        next_copy(0, turn, z).start()
    for step in range(1, cols):
        row_copy(step).start()
    for step in range(1, depth):
        high = (z - step + depth) % depth
        field_arrival(high * width + y).wait_recv()
        for turn in range(1, width):
            next_copy(step, turn, high).start()
    for step in range(depth):
        high = (z - step + depth) % depth
        for turn in range(1, width):
            field_arrival(high * width + (y + turn) % width).wait_recv()
    for step in range(1, cols):
        other = (col - step + cols) % cols
        remote(row_out_ref.at[other], row_out_ref.at[other], row_send.at[step], row_recv.at[other], (row, other)).wait_recv()
    for step in range(1, cols):
        row_copy(step).wait_send()
    for step in range(1, depth):
        field_copy(step).wait_send()
    for step in range(depth):
        for turn in range(1, width):
            next_copy(step, turn, (z - step + depth) % depth).wait_send()
    others(lambda spot: index_copy(spot).wait_send())

    def finish(high):
        others(lambda spot: out_copy(high, spot).wait_send())
        others(lambda spot: reply_copy(high, spot).wait_send())

        @pl.when(high != z)
        def _():
            remote(chain_out_ref.at[high], up_ref.at[high], chain_send.at[high], up_recv.at[high], level((z + 1) % depth)).wait_send()

        @pl.when((high <= z) & (z < depth - 1))
        def _():
            relay_up(high).wait_send()

        @pl.when((high >= z) & (z > 0))
        def _():
            relay_down(high).wait_send()

    levels(near_first, finish)


def local(
    rhs,
    front_factor,
    coupling,
    bound_count,
    sep_owner,
    sep_index,
    sep_rhs,
    sep_factor,
    cell_weight,
    cell_pivot,
):
    rows, cols = lax.axis_size("row"), lax.axis_size("col")
    fronts = rows * cols
    width = max(cols // 2, 1)
    depth = rows // width
    plane = width * cols
    bound = coupling.shape[0]
    pivots, sources = rhs.shape
    sep_size = sep_rhs.shape[0]
    cells = cell_weight.shape[0]
    halves = sep_owner.shape[1]
    slots = bound // halves
    base = 256
    shape = jax.ShapeDtypeStruct
    smem = pl.BlockSpec(memory_space=pltpu.SMEM)
    vmem = pl.BlockSpec(memory_space=pltpu.VMEM)
    found = sep_owner[0][None, :] == jnp.arange(fronts, dtype=jnp.int32)[:, None]
    place = jnp.min(jnp.where(found, jnp.arange(halves, dtype=jnp.int32)[None, :], halves), axis=1)
    table = jnp.pad(sep_index.reshape(halves, 1, slots), ((0, 1), (0, 0), (0, 0)), constant_values=-1)
    dma = pltpu.SemaphoreType.DMA
    block = (sep_size, sources)
    group = (slots, sources)
    sep_potential, row_tile, col_tile = pl.pallas_call(
        functools.partial(whole_kernel, depth),
        out_shape=(
            shape(block, F32),
            shape((cols, cells, sources), BF16),
            shape((rows, cells, sources), BF16),
        ),
        in_specs=[smem] * 3 + [vmem] * 8,
        out_specs=(vmem, vmem, vmem),
        scratch_shapes=[
            pltpu.VMEM((pivots, pivots), BF16),
            pltpu.VMEM((pivots, pivots), BF16),
            pltpu.VMEM((pivots // base, base, base), F32),
            pltpu.VMEM((sep_size, sep_size), BF16),
            pltpu.VMEM((sep_size, sep_size), BF16),
            pltpu.VMEM((sep_size // base, base, base), F32),
            pltpu.VMEM((bound, sources), BF16),
            pltpu.VMEM((halves + 1,) + group, BF16),
            pltpu.VMEM((plane, depth, 1, slots), jnp.int32),
            pltpu.VMEM((plane, depth, 1, slots), jnp.int32),
            pltpu.VMEM((depth, slots, plane), jnp.int32),
            pltpu.VMEM((depth, plane) + group, BF16),
            pltpu.VMEM((depth, plane) + group, BF16),
            pltpu.VMEM((depth,) + block, BF16),
            pltpu.VMEM((depth,) + block, BF16),
            pltpu.VMEM((depth,) + block, BF16),
            pltpu.VMEM(block, F32),
            pltpu.VMEM((depth,) + block, BF16),
            pltpu.VMEM((depth, plane) + group, BF16),
            pltpu.VMEM((fronts,) + group, BF16),
            dma((plane,)),
            dma((plane,)),
            dma((depth, plane)),
            dma((depth, plane)),
            dma((depth,)),
            dma((depth,)),
            dma((depth,)),
            dma((depth,)),
            dma((depth,)),
            dma((depth,)),
            dma((depth, plane)),
            dma((depth, plane)),
            dma((depth,)),
            dma((rows,)),
            dma((depth, width)),
            dma((cols,)),
            dma((cols,)),
        ],
        cost_estimate=pl.CostEstimate(flops=10**10, bytes_accessed=10**7, transcendentals=0),
        compiler_params=pltpu.CompilerParams(vmem_limit_bytes=VMEM_LIMIT, collective_id=0, has_side_effects=True),
    )(bound_count, sep_owner, place, table, front_factor, rhs, coupling, sep_rhs, sep_factor, cell_weight, cell_pivot)
    gram = dot(row_tile.reshape(cols * cells, sources), col_tile.reshape(rows * cells, sources), NT) * (1.0 / sources)
    return (sep_potential, gram * gram)


def solution(mesh):
    both_axes = P(("row", "col"), None)
    placed = (both_axes, both_axes, both_axes, P(("row", "col"))) + (both_axes,) * 6
    return jax.shard_map(
        local,
        mesh=mesh,
        in_specs=placed,
        out_specs=(both_axes, P("row", "col")),
        check_vma=False,
    )
```

```python
import functools

import jax
import jax.numpy as jnp
from jax import lax
from jax.experimental import pallas as pl
from jax.experimental.pallas import tpu as pltpu
from jax.sharding import PartitionSpec as P

F32 = jnp.float32
BF16 = jnp.bfloat16
NN = (((1,), (0,)), ((), ()))
NT = (((1,), (1,)), ((), ()))
VMEM_LIMIT = 63 * 1024 * 1024


def split(value):
    high = value.astype(BF16)
    return high, (value - high.astype(F32)).astype(BF16)


def dot(left, right, dims):
    return lax.dot_general(left, right, dims, preferred_element_type=F32)


def dot3(left, right, dims=NN):
    return dot(left[0], right[0], dims) + (dot(left[0], right[1], dims) + dot(left[1], right[0], dims))


def invert(factor_ref, high_ref, low_ref, work_ref, ready):
    order = factor_ref.shape[0]
    base = work_ref.shape[1]
    count = order // base
    rows = lax.broadcasted_iota(jnp.int32, (base, base), 0)
    cols = lax.broadcasted_iota(jnp.int32, (base, base), 1)
    differ = rows ^ cols
    below = rows > cols
    high_ref[...] = jnp.zeros_like(high_ref)
    low_ref[...] = jnp.zeros_like(low_ref)

    def diagonal(block):
        return factor_ref[pl.ds(block * base, base), pl.ds(block * base, base)]

    for block in range(count):
        ready(block, block)
        part = diagonal(block)
        only = jnp.where(differ == 0, part, 0.0)
        down = 1.0 / jnp.sum(only, axis=1, keepdims=True)
        across = 1.0 / jnp.sum(only, axis=0, keepdims=True)
        pairs = jnp.where(below & (differ == 1), (part * down) * across, 0.0)
        work_ref[block] = jnp.where(differ == 0, jnp.broadcast_to(down, part.shape), -pairs)
    size = 2
    while size < base:
        inside = below & (differ >= size) & (differ < 2 * size)
        for block in range(count):
            outer = split(jnp.where(inside, diagonal(block), 0.0))
            held = work_ref[block]
            parts = split(held)
            step = split(dot3(outer, parts))
            work_ref[block] = held - dot3(parts, step)
        size *= 2
    for block in range(count):
        spot = pl.ds(block * base, base)
        high, low = split(work_ref[block])
        high_ref[spot, spot] = high
        low_ref[spot, spot] = low
    size = base
    while size < order:
        for start in range(0, order, 2 * size):
            first, second = pl.ds(start, size), pl.ds(start + size, size)
            for down in range(size // base):
                for across in range(size // base):
                    ready((start + size) // base + down, start // base + across)
            outer = split(factor_ref[second, first])
            step = split(dot3(outer, (high_ref[first, first], low_ref[first, first])))
            high, low = split(-dot3((high_ref[second, second], low_ref[second, second]), step))
            high_ref[second, first] = high
            low_ref[second, first] = low
        size *= 2


def turned_solve(turned, high_ref, low_ref):
    inverse = (high_ref[...], low_ref[...])
    half_way = split(dot3(split(turned), inverse, NT))
    return dot3(half_way, inverse, NN)


MESH = pl.DeviceIdType.MESH


def whole_kernel(
    depth,
    count_ref,
    owner_ref,
    place_ref,
    table_ref,
    factor_hbm,
    rhs_ref,
    coupling_hbm,
    sep_rhs_ref,
    sep_factor_hbm,
    weight_ref,
    pivot_ref,
    sep_out_ref,
    row_out_ref,
    col_out_ref,
    high_ref,
    low_ref,
    work_ref,
    factor_ref,
    sep_factor_ref,
    coupling_ref,
    sep_high_ref,
    sep_low_ref,
    sep_work_ref,
    flat_ref,
    contrib_ref,
    index_out_ref,
    index_ref,
    column_ref,
    stage_ref,
    received_ref,
    chain_out_ref,
    up_ref,
    down_ref,
    own_ref,
    halves_ref,
    reply_ref,
    returned_ref,
    index_send,
    index_recv,
    out_send,
    out_recv,
    chain_send,
    up_recv,
    down_recv,
    relay_up_send,
    relay_down_send,
    relay_recv,
    reply_send,
    reply_recv,
    field_send,
    field_recv,
    next_send,
    row_send,
    row_recv,
    spread_ref,
    turned_rhs_ref,
    factor_load,
    sep_load,
    coupling_load,
):
    base = work_ref.shape[1]

    def load(source, target, sems, down, across):
        spot = (pl.ds(down * base, base), pl.ds(across * base, base))
        return pltpu.make_async_copy(source.at[spot], target.at[spot], sems.at[down, across])

    def front_block(down, across):
        return load(factor_hbm, factor_ref, factor_load, down, across)

    def sep_block(down, across):
        return load(sep_factor_hbm, sep_factor_ref, sep_load, down, across)

    def each_block(count, action):
        for away in range(count):
            for down in range(away, count):
                action(down, down - away)

    coupling_copy = pltpu.make_async_copy(coupling_hbm, coupling_ref, coupling_load)
    each_block(work_ref.shape[0], lambda down, across: front_block(down, across).start())
    coupling_copy.start()
    each_block(sep_work_ref.shape[0], lambda down, across: sep_block(down, across).start())
    rows, cols = col_out_ref.shape[0], row_out_ref.shape[0]
    width = rows // depth
    plane = width * cols
    row, col = lax.axis_index("row"), lax.axis_index("col")
    z, y = row // width, row % width
    me = y * cols + col
    halves, slots = owner_ref.shape[1], table_ref.shape[2]
    sep_size = sep_rhs_ref.shape[0]

    def peer(spot):
        return (z * width + spot // cols, spot % cols)

    def level(spot):
        return (spot * width + y, col)

    barrier = pltpu.get_barrier_semaphore()
    for step in range(1, plane):
        pl.semaphore_signal(barrier, inc=1, device_id=peer((me + step) % plane), device_id_type=MESH)
    for step in range(1, depth):
        pl.semaphore_signal(barrier, inc=1, device_id=level((z + step) % depth), device_id_type=MESH)

    def remote(source, target, send, recv, device):
        return pltpu.make_async_remote_copy(
            src_ref=source, dst_ref=target, send_sem=send, recv_sem=recv, device_id=device, device_id_type=MESH
        )

    def index_copy(spot):
        return remote(index_out_ref.at[spot], index_ref.at[me], index_send.at[spot], index_recv.at[me], peer(spot))

    def index_arrival(spot):
        return remote(index_out_ref.at[spot], index_ref.at[spot], index_send.at[spot], index_recv.at[spot], peer(spot))

    def out_copy(high, spot):
        return remote(
            stage_ref.at[high, spot], received_ref.at[high, me], out_send.at[high, spot], out_recv.at[high, me], peer(spot)
        )

    def out_arrival(high, spot):
        return remote(
            stage_ref.at[high, spot], received_ref.at[high, spot], out_send.at[high, spot], out_recv.at[high, spot], peer(spot)
        )

    def up_copy(high):
        return remote(chain_out_ref.at[high], up_ref.at[high], chain_send.at[high], up_recv.at[high], level(z + 1))

    def down_copy(high):
        return remote(chain_out_ref.at[high], down_ref.at[high], chain_send.at[high], down_recv.at[high], level(z - 1))

    def relay_up(high):
        return remote(halves_ref.at[high], halves_ref.at[high], relay_up_send.at[high], relay_recv.at[high], level(z + 1))

    def relay_down(high):
        return remote(halves_ref.at[high], halves_ref.at[high], relay_down_send.at[high], relay_recv.at[high], level(z - 1))

    def reply_copy(high, spot):
        return remote(
            reply_ref.at[high, spot], returned_ref.at[high * plane + me], reply_send.at[high, spot], reply_recv.at[high, me], peer(spot)
        )

    def reply_arrival(high, spot):
        return remote(
            reply_ref.at[high, spot], returned_ref.at[high * plane + spot], reply_send.at[high, spot], reply_recv.at[high, spot], peer(spot)
        )

    def others(action):
        def step(offset, carry):
            action((me + offset) % plane)
            return carry

        lax.fori_loop(1, plane, step, 0)

    def levels(order, action):
        def step(at, carry):
            spot = order(at)

            @pl.when((spot >= 0) & (spot < depth))
            def _():
                action(spot)

            return carry

        lax.fori_loop(0, 2 * depth - 1, step, 0)

    def far_first(at):
        distance = depth - 1 - at // 2
        return z + distance * (1 - 2 * (at % 2))

    def near_first(at):
        return z + ((at + 1) // 2) * (1 - 2 * (at % 2))

    invert(factor_ref, high_ref, low_ref, work_ref, lambda down, across: front_block(down, across).wait())
    pl.semaphore_wait(barrier, plane + depth - 2)

    def fill_index(spot, carry):
        for high in range(depth):
            index_out_ref[spot, high] = table_ref[place_ref[high * plane + spot]]
        return carry

    lax.fori_loop(0, plane, fill_index, 0)
    others(lambda spot: index_copy(spot).start())
    index_ref[me] = index_out_ref[me]

    turned_rhs = rhs_ref[...].T
    solved = turned_solve(turned_rhs, high_ref, low_ref).astype(BF16)
    coupling_copy.wait()
    product = dot(coupling_ref[...], solved, NT)
    live = lax.broadcasted_iota(jnp.int32, product.shape, 0) < count_ref[0]
    flat_ref[...] = jnp.where(live, product, 0.0).astype(BF16)
    for half in range(halves):
        contrib_ref[half] = flat_ref[pl.ds(half * slots, slots), :]
    contrib_ref[halves] = jnp.zeros(contrib_ref.shape[1:], BF16)

    def send_out(high):
        def one(spot):
            stage_ref[high, spot] = contrib_ref[place_ref[high * plane + spot]]
            out_copy(high, spot).start()

        others(one)
        received_ref[high, me] = contrib_ref[place_ref[high * plane + me]]

    levels(far_first, send_out)
    invert(sep_factor_ref, sep_high_ref, sep_low_ref, sep_work_ref, lambda down, across: sep_block(down, across).wait())
    others(lambda spot: index_arrival(spot).wait_recv())
    for high in range(depth):
        column_ref[high] = jnp.concatenate([index_ref[spot, high] for spot in range(plane)], axis=0).T

    def gather_in(high):
        others(lambda spot: out_arrival(high, spot).wait_recv())
        numbers = lax.broadcasted_iota(jnp.int32, (sep_size, slots), 0)
        own_ref[...] = jnp.zeros_like(own_ref)
        for spot in range(plane):
            selector = jnp.where(numbers == index_ref[spot, high], 1.0, 0.0).astype(BF16)
            own_ref[...] += dot(selector, received_ref[high, spot], NN)

        @pl.when((high >= z) & (z > 0))
        def _():
            remote(chain_out_ref.at[high], up_ref.at[high], chain_send.at[high], up_recv.at[high], level(z - 1)).wait_recv()
            own_ref[...] += up_ref[high].astype(F32)

        @pl.when((high <= z) & (z < depth - 1))
        def _():
            remote(chain_out_ref.at[high], down_ref.at[high], chain_send.at[high], down_recv.at[high], level(z + 1)).wait_recv()
            own_ref[...] += down_ref[high].astype(F32)

        @pl.when(high != z)
        def _():
            chain_out_ref[high] = own_ref[...].astype(BF16)

        @pl.when(high > z)
        def _():
            up_copy(high).start()

        @pl.when(high < z)
        def _():
            down_copy(high).start()

    levels(far_first, gather_in)
    reduced = (sep_rhs_ref[...] - own_ref[...]).T
    potential = turned_solve(reduced, sep_high_ref, sep_low_ref).T
    sep_out_ref[...] = potential
    halves_ref[z] = potential.astype(BF16)

    def pass_on(high):
        @pl.when(high != z)
        def _():
            remote(halves_ref.at[high], halves_ref.at[high], relay_up_send.at[high], relay_recv.at[high], level((z + 1) % depth)).wait_recv()

        @pl.when((high <= z) & (z < depth - 1))
        def _():
            relay_up(high).start()

        @pl.when((high >= z) & (z > 0))
        def _():
            relay_down(high).start()

        numbers = lax.broadcasted_iota(jnp.int32, (slots, sep_size), 1)
        for spot in range(plane):
            picker = jnp.where(numbers == column_ref[high, :, spot : spot + 1], 1.0, 0.0).astype(BF16)
            reply_ref[high, spot] = dot(picker, halves_ref[high], NN).astype(BF16)

            @pl.when(me != spot)
            def _():
                reply_copy(high, spot).start()

        returned_ref[high * plane + me] = reply_ref[high, me]

    levels(near_first, pass_on)
    weight, pivot = weight_ref[...].T, pivot_ref[...].T
    shape = (weight.shape[0], rhs_ref.shape[0])
    spots = lax.broadcasted_iota(jnp.int32, shape, 1)
    spread = jnp.zeros(shape, F32)
    for near in range(weight.shape[1]):
        spread += jnp.where(spots == pivot[:, near : near + 1], weight[:, near : near + 1], 0.0)
    spread_high, spread_low = split(spread)
    spread_ref[0], spread_ref[1] = spread_high, spread_low
    turned_rhs_ref[...] = rhs_ref[...].T
    levels(near_first, lambda high: others(lambda spot: reply_arrival(high, spot).wait_recv()))
    for half in range(halves):
        flat_ref[pl.ds(half * slots, slots), :] = returned_ref[owner_ref[0, half]]
    values = flat_ref[...]
    live = lax.broadcasted_iota(jnp.int32, values.shape, 0) < count_ref[0]
    values = jnp.where(live, values.astype(F32), 0.0).astype(BF16)
    lifted = dot(values.T, coupling_ref[...], NN)
    potential = turned_solve(turned_rhs_ref[...] - lifted, high_ref, low_ref)
    field = dot3((spread_ref[0], spread_ref[1]), split(potential), NT).astype(BF16)
    col_out_ref[row] = field
    row_out_ref[col] = field

    def field_copy(step):
        return remote(
            col_out_ref.at[row], col_out_ref.at[row], field_send.at[step], field_recv.at[row], level((z + step) % depth)
        )

    def next_copy(step, turn, high):
        spot = high * width + y
        target = (z * width + (y + turn) % width, col)
        return remote(col_out_ref.at[spot], col_out_ref.at[spot], next_send.at[step, turn], field_recv.at[spot], target)

    def row_copy(step):
        return remote(
            row_out_ref.at[col], row_out_ref.at[col], row_send.at[step], row_recv.at[col], (row, (col + step) % cols)
        )

    def field_arrival(spot):
        return remote(col_out_ref.at[spot], col_out_ref.at[spot], field_send.at[0], field_recv.at[spot], level((z + 1) % depth))

    for step in range(1, depth):
        field_copy(step).start()
    for turn in range(1, width):
        next_copy(0, turn, z).start()
    for step in range(1, cols):
        row_copy(step).start()
    for step in range(1, depth):
        high = (z - step + depth) % depth
        field_arrival(high * width + y).wait_recv()
        for turn in range(1, width):
            next_copy(step, turn, high).start()
    for step in range(depth):
        high = (z - step + depth) % depth
        for turn in range(1, width):
            field_arrival(high * width + (y + turn) % width).wait_recv()
    for step in range(1, cols):
        other = (col - step + cols) % cols
        remote(row_out_ref.at[other], row_out_ref.at[other], row_send.at[step], row_recv.at[other], (row, other)).wait_recv()
    for step in range(1, cols):
        row_copy(step).wait_send()
    for step in range(1, depth):
        field_copy(step).wait_send()
    for step in range(depth):
        for turn in range(1, width):
            next_copy(step, turn, (z - step + depth) % depth).wait_send()
    others(lambda spot: index_copy(spot).wait_send())

    def finish(high):
        others(lambda spot: out_copy(high, spot).wait_send())
        others(lambda spot: reply_copy(high, spot).wait_send())

        @pl.when(high != z)
        def _():
            remote(chain_out_ref.at[high], up_ref.at[high], chain_send.at[high], up_recv.at[high], level((z + 1) % depth)).wait_send()

        @pl.when((high <= z) & (z < depth - 1))
        def _():
            relay_up(high).wait_send()

        @pl.when((high >= z) & (z > 0))
        def _():
            relay_down(high).wait_send()

    levels(near_first, finish)


def local(
    rhs,
    front_factor,
    coupling,
    bound_count,
    sep_owner,
    sep_index,
    sep_rhs,
    sep_factor,
    cell_weight,
    cell_pivot,
):
    rows, cols = lax.axis_size("row"), lax.axis_size("col")
    fronts = rows * cols
    width = max(cols // 2, 1)
    depth = rows // width
    plane = width * cols
    bound = coupling.shape[0]
    pivots, sources = rhs.shape
    sep_size = sep_rhs.shape[0]
    cells = cell_weight.shape[0]
    halves = sep_owner.shape[1]
    slots = bound // halves
    base = 256
    shape = jax.ShapeDtypeStruct
    smem = pl.BlockSpec(memory_space=pltpu.SMEM)
    vmem = pl.BlockSpec(memory_space=pltpu.VMEM)
    hbm = pl.BlockSpec(memory_space=pl.ANY)
    found = sep_owner[0][None, :] == jnp.arange(fronts, dtype=jnp.int32)[:, None]
    place = jnp.min(jnp.where(found, jnp.arange(halves, dtype=jnp.int32)[None, :], halves), axis=1)
    table = jnp.pad(sep_index.reshape(halves, 1, slots), ((0, 1), (0, 0), (0, 0)), constant_values=-1)
    dma = pltpu.SemaphoreType.DMA
    block = (sep_size, sources)
    group = (slots, sources)
    sep_potential, row_tile, col_tile = pl.pallas_call(
        functools.partial(whole_kernel, depth),
        out_shape=(
            shape(block, F32),
            shape((cols, cells, sources), BF16),
            shape((rows, cells, sources), BF16),
        ),
        in_specs=[smem] * 3 + [vmem, hbm, vmem, hbm, vmem, hbm, vmem, vmem],
        out_specs=(vmem, vmem, vmem),
        scratch_shapes=[
            pltpu.VMEM((pivots, pivots), BF16),
            pltpu.VMEM((pivots, pivots), BF16),
            pltpu.VMEM((pivots // base, base, base), F32),
            pltpu.VMEM((pivots, pivots), F32),
            pltpu.VMEM((sep_size, sep_size), F32),
            pltpu.VMEM((bound, pivots), BF16),
            pltpu.VMEM((sep_size, sep_size), BF16),
            pltpu.VMEM((sep_size, sep_size), BF16),
            pltpu.VMEM((sep_size // base, base, base), F32),
            pltpu.VMEM((bound, sources), BF16),
            pltpu.VMEM((halves + 1,) + group, BF16),
            pltpu.VMEM((plane, depth, 1, slots), jnp.int32),
            pltpu.VMEM((plane, depth, 1, slots), jnp.int32),
            pltpu.VMEM((depth, slots, plane), jnp.int32),
            pltpu.VMEM((depth, plane) + group, BF16),
            pltpu.VMEM((depth, plane) + group, BF16),
            pltpu.VMEM((depth,) + block, BF16),
            pltpu.VMEM((depth,) + block, BF16),
            pltpu.VMEM((depth,) + block, BF16),
            pltpu.VMEM(block, F32),
            pltpu.VMEM((depth,) + block, BF16),
            pltpu.VMEM((depth, plane) + group, BF16),
            pltpu.VMEM((fronts,) + group, BF16),
            dma((plane,)),
            dma((plane,)),
            dma((depth, plane)),
            dma((depth, plane)),
            dma((depth,)),
            dma((depth,)),
            dma((depth,)),
            dma((depth,)),
            dma((depth,)),
            dma((depth,)),
            dma((depth, plane)),
            dma((depth, plane)),
            dma((depth,)),
            dma((rows,)),
            dma((depth, width)),
            dma((cols,)),
            dma((cols,)),
            pltpu.VMEM((2, cells, pivots), BF16),
            pltpu.VMEM((sources, pivots), F32),
            dma((pivots // base, pivots // base)),
            dma((sep_size // base, sep_size // base)),
            dma,
        ],
        cost_estimate=pl.CostEstimate(flops=10**10, bytes_accessed=10**7, transcendentals=0),
        compiler_params=pltpu.CompilerParams(vmem_limit_bytes=VMEM_LIMIT, collective_id=0, has_side_effects=True),
    )(bound_count, sep_owner, place, table, front_factor, rhs, coupling, sep_rhs, sep_factor, cell_weight.T, cell_pivot.T)
    gram = dot(row_tile.reshape(cols * cells, sources), col_tile.reshape(rows * cells, sources), NT) * (1.0 / sources)
    return (sep_potential, gram * gram)


def solution(mesh):
    both_axes = P(("row", "col"), None)
    placed = (both_axes, both_axes, both_axes, P(("row", "col"))) + (both_axes,) * 6
    return jax.shard_map(
        local,
        mesh=mesh,
        in_specs=placed,
        out_specs=(both_axes, P("row", "col")),
        check_vma=False,
    )
```

```python
import functools

import jax
import jax.numpy as jnp
from jax import lax
from jax.experimental import pallas as pl
from jax.experimental.pallas import tpu as pltpu
from jax.sharding import PartitionSpec as P

F32 = jnp.float32
BF16 = jnp.bfloat16
NN = (((1,), (0,)), ((), ()))
NT = (((1,), (1,)), ((), ()))
VMEM_LIMIT = 63 * 1024 * 1024


def split(value):
    high = value.astype(BF16)
    return high, (value - high.astype(F32)).astype(BF16)


def dot(left, right, dims):
    return lax.dot_general(left, right, dims, preferred_element_type=F32)


def dot3(left, right, dims=NN):
    return dot(left[0], right[0], dims) + (dot(left[0], right[1], dims) + dot(left[1], right[0], dims))


def invert(factor_ref, high_ref, low_ref, work_ref, ready):
    order = factor_ref.shape[0]
    base = work_ref.shape[1]
    count = order // base
    rows = lax.broadcasted_iota(jnp.int32, (base, base), 0)
    cols = lax.broadcasted_iota(jnp.int32, (base, base), 1)
    differ = rows ^ cols
    below = rows > cols
    high_ref[...] = jnp.zeros_like(high_ref)
    low_ref[...] = jnp.zeros_like(low_ref)

    def diagonal(block):
        return factor_ref[pl.ds(block * base, base), pl.ds(block * base, base)]

    for block in range(count):
        ready(block, block)
        part = diagonal(block)
        only = jnp.where(differ == 0, part, 0.0)
        down = 1.0 / jnp.sum(only, axis=1, keepdims=True)
        across = 1.0 / jnp.sum(only, axis=0, keepdims=True)
        pairs = jnp.where(below & (differ == 1), (part * down) * across, 0.0)
        work_ref[block] = jnp.where(differ == 0, jnp.broadcast_to(down, part.shape), -pairs)
    size = 2
    while size < base:
        inside = below & (differ >= size) & (differ < 2 * size)
        for block in range(count):
            outer = split(jnp.where(inside, diagonal(block), 0.0))
            held = work_ref[block]
            parts = split(held)
            step = split(dot3(outer, parts))
            work_ref[block] = held - dot3(parts, step)
        size *= 2
    for block in range(count):
        spot = pl.ds(block * base, base)
        high, low = split(work_ref[block])
        high_ref[spot, spot] = high
        low_ref[spot, spot] = low
    size = base
    while size < order:
        for start in range(0, order, 2 * size):
            first, second = pl.ds(start, size), pl.ds(start + size, size)
            for down in range(size // base):
                for across in range(size // base):
                    ready((start + size) // base + down, start // base + across)
            outer = split(factor_ref[second, first])
            step = split(dot3(outer, (high_ref[first, first], low_ref[first, first])))
            high, low = split(-dot3((high_ref[second, second], low_ref[second, second]), step))
            high_ref[second, first] = high
            low_ref[second, first] = low
        size *= 2


def turned_solve(turned, high_ref, low_ref):
    inverse = (high_ref[...], low_ref[...])
    half_way = split(dot3(split(turned), inverse, NT))
    return dot3(half_way, inverse, NN)


MESH = pl.DeviceIdType.MESH


def whole_kernel(
    depth,
    count_ref,
    owner_ref,
    place_ref,
    table_ref,
    factor_hbm,
    rhs_ref,
    coupling_hbm,
    sep_rhs_ref,
    sep_factor_hbm,
    weight_ref,
    pivot_ref,
    sep_out_ref,
    row_out_ref,
    col_out_ref,
    high_ref,
    low_ref,
    work_ref,
    factor_ref,
    sep_factor_ref,
    coupling_ref,
    sep_high_ref,
    sep_low_ref,
    sep_work_ref,
    flat_ref,
    contrib_ref,
    index_out_ref,
    index_ref,
    column_ref,
    stage_ref,
    received_ref,
    chain_out_ref,
    up_ref,
    down_ref,
    own_ref,
    halves_ref,
    reply_ref,
    returned_ref,
    index_send,
    index_recv,
    out_send,
    out_recv,
    chain_send,
    up_recv,
    down_recv,
    relay_up_send,
    relay_down_send,
    relay_recv,
    reply_send,
    reply_recv,
    field_send,
    field_recv,
    next_send,
    row_send,
    row_recv,
    spread_ref,
    turned_rhs_ref,
    factor_load,
    sep_load,
    coupling_load,
):
    base = work_ref.shape[1]

    def load(source, target, sems, down, across):
        spot = (pl.ds(down * base, base), pl.ds(across * base, base))
        return pltpu.make_async_copy(source.at[spot], target.at[spot], sems.at[down, across])

    def front_block(down, across):
        return load(factor_hbm, factor_ref, factor_load, down, across)

    def sep_block(down, across):
        return load(sep_factor_hbm, sep_factor_ref, sep_load, down, across)

    def each_block(count, action):
        for away in range(count):
            for down in range(away, count):
                action(down, down - away)

    coupling_copy = pltpu.make_async_copy(coupling_hbm, coupling_ref, coupling_load)
    each_block(work_ref.shape[0], lambda down, across: front_block(down, across).start())
    coupling_copy.start()
    each_block(sep_work_ref.shape[0], lambda down, across: sep_block(down, across).start())
    rows, cols = col_out_ref.shape[0], row_out_ref.shape[0]
    width = rows // depth
    plane = width * cols
    row, col = lax.axis_index("row"), lax.axis_index("col")
    z, y = row // width, row % width
    me = y * cols + col
    halves, slots = owner_ref.shape[1], table_ref.shape[2]
    sep_size = sep_rhs_ref.shape[0]

    def peer(spot):
        return (z * width + spot // cols, spot % cols)

    def level(spot):
        return (spot * width + y, col)

    barrier = pltpu.get_barrier_semaphore()
    for step in range(1, plane):
        pl.semaphore_signal(barrier, inc=1, device_id=peer((me + step) % plane), device_id_type=MESH)
    for step in range(1, depth):
        pl.semaphore_signal(barrier, inc=1, device_id=level((z + step) % depth), device_id_type=MESH)

    def remote(source, target, send, recv, device):
        return pltpu.make_async_remote_copy(
            src_ref=source, dst_ref=target, send_sem=send, recv_sem=recv, device_id=device, device_id_type=MESH
        )

    def index_copy(spot):
        return remote(index_out_ref.at[spot], index_ref.at[me], index_send.at[spot], index_recv.at[me], peer(spot))

    def index_arrival(spot):
        return remote(index_out_ref.at[spot], index_ref.at[spot], index_send.at[spot], index_recv.at[spot], peer(spot))

    def out_copy(high, spot):
        return remote(
            stage_ref.at[high, spot], received_ref.at[high, me], out_send.at[high, spot], out_recv.at[high, me], peer(spot)
        )

    def out_arrival(high, spot):
        return remote(
            stage_ref.at[high, spot], received_ref.at[high, spot], out_send.at[high, spot], out_recv.at[high, spot], peer(spot)
        )

    def up_copy(high):
        return remote(chain_out_ref.at[high], up_ref.at[high], chain_send.at[high], up_recv.at[high], level(z + 1))

    def down_copy(high):
        return remote(chain_out_ref.at[high], down_ref.at[high], chain_send.at[high], down_recv.at[high], level(z - 1))

    def relay_up(high):
        return remote(halves_ref.at[high], halves_ref.at[high], relay_up_send.at[high], relay_recv.at[high], level(z + 1))

    def relay_down(high):
        return remote(halves_ref.at[high], halves_ref.at[high], relay_down_send.at[high], relay_recv.at[high], level(z - 1))

    def reply_copy(high, spot):
        return remote(
            reply_ref.at[high, spot], returned_ref.at[high * plane + me], reply_send.at[high, spot], reply_recv.at[high, me], peer(spot)
        )

    def reply_arrival(high, spot):
        return remote(
            reply_ref.at[high, spot], returned_ref.at[high * plane + spot], reply_send.at[high, spot], reply_recv.at[high, spot], peer(spot)
        )

    def others(action):
        def step(offset, carry):
            action((me + offset) % plane)
            return carry

        lax.fori_loop(1, plane, step, 0)

    def levels(order, action):
        def step(at, carry):
            spot = order(at)

            @pl.when((spot >= 0) & (spot < depth))
            def _():
                action(spot)

            return carry

        lax.fori_loop(0, 2 * depth - 1, step, 0)

    def far_first(at):
        distance = depth - 1 - at // 2
        return z + distance * (1 - 2 * (at % 2))

    def near_first(at):
        return z + ((at + 1) // 2) * (1 - 2 * (at % 2))

    invert(factor_ref, high_ref, low_ref, work_ref, lambda down, across: front_block(down, across).wait())
    pl.semaphore_wait(barrier, plane + depth - 2)

    def fill_index(spot, carry):
        for high in range(depth):
            index_out_ref[spot, high] = table_ref[place_ref[high * plane + spot]]
        return carry

    lax.fori_loop(0, plane, fill_index, 0)
    others(lambda spot: index_copy(spot).start())
    index_ref[me] = index_out_ref[me]

    turned_rhs = rhs_ref[...].T
    solved = turned_solve(turned_rhs, high_ref, low_ref).astype(BF16)
    coupling_copy.wait()
    product = dot(coupling_ref[...], solved, NT)
    live = lax.broadcasted_iota(jnp.int32, product.shape, 0) < count_ref[0]
    flat_ref[...] = jnp.where(live, product, 0.0).astype(BF16)
    for half in range(halves):
        contrib_ref[half] = flat_ref[pl.ds(half * slots, slots), :]
    contrib_ref[halves] = jnp.zeros(contrib_ref.shape[1:], BF16)

    def send_out(high):
        def one(spot):
            stage_ref[high, spot] = contrib_ref[place_ref[high * plane + spot]]
            out_copy(high, spot).start()

        others(one)
        received_ref[high, me] = contrib_ref[place_ref[high * plane + me]]

    levels(far_first, send_out)
    invert(sep_factor_ref, sep_high_ref, sep_low_ref, sep_work_ref, lambda down, across: sep_block(down, across).wait())
    others(lambda spot: index_arrival(spot).wait_recv())
    for high in range(depth):
        column_ref[high] = jnp.concatenate([index_ref[spot, high] for spot in range(plane)], axis=0).T

    def gather_in(high):
        numbers = lax.broadcasted_iota(jnp.int32, (sep_size, slots), 0)
        own_ref[...] = jnp.zeros_like(own_ref)
        for spot in range(plane):

            @pl.when(me != spot)
            def _():
                out_arrival(high, spot).wait_recv()

            selector = jnp.where(numbers == index_ref[spot, high], 1.0, 0.0).astype(BF16)
            own_ref[...] += dot(selector, received_ref[high, spot], NN)

        @pl.when((high >= z) & (z > 0))
        def _():
            remote(chain_out_ref.at[high], up_ref.at[high], chain_send.at[high], up_recv.at[high], level(z - 1)).wait_recv()
            own_ref[...] += up_ref[high].astype(F32)

        @pl.when((high <= z) & (z < depth - 1))
        def _():
            remote(chain_out_ref.at[high], down_ref.at[high], chain_send.at[high], down_recv.at[high], level(z + 1)).wait_recv()
            own_ref[...] += down_ref[high].astype(F32)

        @pl.when(high != z)
        def _():
            chain_out_ref[high] = own_ref[...].astype(BF16)

        @pl.when(high > z)
        def _():
            up_copy(high).start()

        @pl.when(high < z)
        def _():
            down_copy(high).start()

    levels(far_first, gather_in)
    reduced = (sep_rhs_ref[...] - own_ref[...]).T
    potential = turned_solve(reduced, sep_high_ref, sep_low_ref).T
    sep_out_ref[...] = potential
    halves_ref[z] = potential.astype(BF16)

    def pass_on(high):
        @pl.when(high != z)
        def _():
            remote(halves_ref.at[high], halves_ref.at[high], relay_up_send.at[high], relay_recv.at[high], level((z + 1) % depth)).wait_recv()

        @pl.when((high <= z) & (z < depth - 1))
        def _():
            relay_up(high).start()

        @pl.when((high >= z) & (z > 0))
        def _():
            relay_down(high).start()

        numbers = lax.broadcasted_iota(jnp.int32, (slots, sep_size), 1)
        for spot in range(plane):
            picker = jnp.where(numbers == column_ref[high, :, spot : spot + 1], 1.0, 0.0).astype(BF16)
            reply_ref[high, spot] = dot(picker, halves_ref[high], NN).astype(BF16)

            @pl.when(me != spot)
            def _():
                reply_copy(high, spot).start()

        returned_ref[high * plane + me] = reply_ref[high, me]

    levels(near_first, pass_on)
    weight, pivot = weight_ref[...].T, pivot_ref[...].T
    shape = (weight.shape[0], rhs_ref.shape[0])
    spots = lax.broadcasted_iota(jnp.int32, shape, 1)
    spread = jnp.zeros(shape, F32)
    for near in range(weight.shape[1]):
        spread += jnp.where(spots == pivot[:, near : near + 1], weight[:, near : near + 1], 0.0)
    spread_high, spread_low = split(spread)
    spread_ref[0], spread_ref[1] = spread_high, spread_low
    turned_rhs_ref[...] = rhs_ref[...].T
    levels(near_first, lambda high: others(lambda spot: reply_arrival(high, spot).wait_recv()))
    for half in range(halves):
        flat_ref[pl.ds(half * slots, slots), :] = returned_ref[owner_ref[0, half]]
    values = flat_ref[...]
    live = lax.broadcasted_iota(jnp.int32, values.shape, 0) < count_ref[0]
    values = jnp.where(live, values.astype(F32), 0.0).astype(BF16)
    lifted = dot(values.T, coupling_ref[...], NN)
    potential = turned_solve(turned_rhs_ref[...] - lifted, high_ref, low_ref)
    field = dot3((spread_ref[0], spread_ref[1]), split(potential), NT).astype(BF16)
    col_out_ref[row] = field
    row_out_ref[col] = field

    def field_copy(step):
        return remote(
            col_out_ref.at[row], col_out_ref.at[row], field_send.at[step], field_recv.at[row], level((z + step) % depth)
        )

    def next_copy(step, turn, high):
        spot = high * width + y
        target = (z * width + (y + turn) % width, col)
        return remote(col_out_ref.at[spot], col_out_ref.at[spot], next_send.at[step, turn], field_recv.at[spot], target)

    def row_copy(step):
        return remote(
            row_out_ref.at[col], row_out_ref.at[col], row_send.at[step], row_recv.at[col], (row, (col + step) % cols)
        )

    def field_arrival(spot):
        return remote(col_out_ref.at[spot], col_out_ref.at[spot], field_send.at[0], field_recv.at[spot], level((z + 1) % depth))

    for step in range(1, depth):
        field_copy(step).start()
    for turn in range(1, width):
        next_copy(0, turn, z).start()
    for step in range(1, cols):
        row_copy(step).start()
    for step in range(1, depth):
        high = (z - step + depth) % depth
        field_arrival(high * width + y).wait_recv()
        for turn in range(1, width):
            next_copy(step, turn, high).start()
    for step in range(depth):
        high = (z - step + depth) % depth
        for turn in range(1, width):
            field_arrival(high * width + (y + turn) % width).wait_recv()
    for step in range(1, cols):
        other = (col - step + cols) % cols
        remote(row_out_ref.at[other], row_out_ref.at[other], row_send.at[step], row_recv.at[other], (row, other)).wait_recv()
    for step in range(1, cols):
        row_copy(step).wait_send()
    for step in range(1, depth):
        field_copy(step).wait_send()
    for step in range(depth):
        for turn in range(1, width):
            next_copy(step, turn, (z - step + depth) % depth).wait_send()
    others(lambda spot: index_copy(spot).wait_send())

    def finish(high):
        others(lambda spot: out_copy(high, spot).wait_send())
        others(lambda spot: reply_copy(high, spot).wait_send())

        @pl.when(high != z)
        def _():
            remote(chain_out_ref.at[high], up_ref.at[high], chain_send.at[high], up_recv.at[high], level((z + 1) % depth)).wait_send()

        @pl.when((high <= z) & (z < depth - 1))
        def _():
            relay_up(high).wait_send()

        @pl.when((high >= z) & (z > 0))
        def _():
            relay_down(high).wait_send()

    levels(near_first, finish)


def local(
    rhs,
    front_factor,
    coupling,
    bound_count,
    sep_owner,
    sep_index,
    sep_rhs,
    sep_factor,
    cell_weight,
    cell_pivot,
):
    rows, cols = lax.axis_size("row"), lax.axis_size("col")
    fronts = rows * cols
    width = max(cols // 2, 1)
    depth = rows // width
    plane = width * cols
    bound = coupling.shape[0]
    pivots, sources = rhs.shape
    sep_size = sep_rhs.shape[0]
    cells = cell_weight.shape[0]
    halves = sep_owner.shape[1]
    slots = bound // halves
    base = 256
    shape = jax.ShapeDtypeStruct
    smem = pl.BlockSpec(memory_space=pltpu.SMEM)
    vmem = pl.BlockSpec(memory_space=pltpu.VMEM)
    hbm = pl.BlockSpec(memory_space=pl.ANY)
    found = sep_owner[0][None, :] == jnp.arange(fronts, dtype=jnp.int32)[:, None]
    place = jnp.min(jnp.where(found, jnp.arange(halves, dtype=jnp.int32)[None, :], halves), axis=1)
    table = jnp.pad(sep_index.reshape(halves, 1, slots), ((0, 1), (0, 0), (0, 0)), constant_values=-1)
    dma = pltpu.SemaphoreType.DMA
    block = (sep_size, sources)
    group = (slots, sources)
    sep_potential, row_tile, col_tile = pl.pallas_call(
        functools.partial(whole_kernel, depth),
        out_shape=(
            shape(block, F32),
            shape((cols, cells, sources), BF16),
            shape((rows, cells, sources), BF16),
        ),
        in_specs=[smem] * 3 + [vmem, hbm, vmem, hbm, vmem, hbm, vmem, vmem],
        out_specs=(vmem, vmem, vmem),
        scratch_shapes=[
            pltpu.VMEM((pivots, pivots), BF16),
            pltpu.VMEM((pivots, pivots), BF16),
            pltpu.VMEM((pivots // base, base, base), F32),
            pltpu.VMEM((pivots, pivots), F32),
            pltpu.VMEM((sep_size, sep_size), F32),
            pltpu.VMEM((bound, pivots), BF16),
            pltpu.VMEM((sep_size, sep_size), BF16),
            pltpu.VMEM((sep_size, sep_size), BF16),
            pltpu.VMEM((sep_size // base, base, base), F32),
            pltpu.VMEM((bound, sources), BF16),
            pltpu.VMEM((halves + 1,) + group, BF16),
            pltpu.VMEM((plane, depth, 1, slots), jnp.int32),
            pltpu.VMEM((plane, depth, 1, slots), jnp.int32),
            pltpu.VMEM((depth, slots, plane), jnp.int32),
            pltpu.VMEM((depth, plane) + group, BF16),
            pltpu.VMEM((depth, plane) + group, BF16),
            pltpu.VMEM((depth,) + block, BF16),
            pltpu.VMEM((depth,) + block, BF16),
            pltpu.VMEM((depth,) + block, BF16),
            pltpu.VMEM(block, F32),
            pltpu.VMEM((depth,) + block, BF16),
            pltpu.VMEM((depth, plane) + group, BF16),
            pltpu.VMEM((fronts,) + group, BF16),
            dma((plane,)),
            dma((plane,)),
            dma((depth, plane)),
            dma((depth, plane)),
            dma((depth,)),
            dma((depth,)),
            dma((depth,)),
            dma((depth,)),
            dma((depth,)),
            dma((depth,)),
            dma((depth, plane)),
            dma((depth, plane)),
            dma((depth,)),
            dma((rows,)),
            dma((depth, width)),
            dma((cols,)),
            dma((cols,)),
            pltpu.VMEM((2, cells, pivots), BF16),
            pltpu.VMEM((sources, pivots), F32),
            dma((pivots // base, pivots // base)),
            dma((sep_size // base, sep_size // base)),
            dma,
        ],
        cost_estimate=pl.CostEstimate(flops=10**10, bytes_accessed=10**7, transcendentals=0),
        compiler_params=pltpu.CompilerParams(vmem_limit_bytes=VMEM_LIMIT, collective_id=0, has_side_effects=True),
    )(bound_count, sep_owner, place, table, front_factor, rhs, coupling, sep_rhs, sep_factor, cell_weight.T, cell_pivot.T)
    gram = dot(row_tile.reshape(cols * cells, sources), col_tile.reshape(rows * cells, sources), NT) * (1.0 / sources)
    return (sep_potential, gram * gram)


def solution(mesh):
    both_axes = P(("row", "col"), None)
    placed = (both_axes, both_axes, both_axes, P(("row", "col"))) + (both_axes,) * 6
    return jax.shard_map(
        local,
        mesh=mesh,
        in_specs=placed,
        out_specs=(both_axes, P("row", "col")),
        check_vma=False,
    )
```
